32 devices in a mesh: graph: 8 (over z, x), dp: 4 (over y, core).
Axes of the slice: x: 2, y: 2, z: 4, core: 2. Of those that a mesh axis runs over, the one named last changes fastest.
Arguments:
- node_state: bfloat16 [4, 4096, 512], P('dp', 'graph'), may hold values from -6 to 6
- edge_state: bfloat16 [4, 16384, 512], P('dp', 'graph'), may hold values from -6 to 6
- senders: int32 [4, 16384], P('dp', 'graph'), may hold values from 0 to 575
- receivers: int32 [4, 16384], P('dp', 'graph'), may hold values from 0 to 511
- send_index: int32 [4, 8, 64], P('dp', 'graph'), may hold values from 0 to 511
- cotangent: bfloat16 [4, 4096, 512], P('dp', 'graph'), may hold values from -0.09375 to 0.09375
- w_edge: bfloat16 [1536, 512], replicated, may hold values from -0.15625 to 0.15625
- w_node: bfloat16 [1024, 512], replicated, may hold values from -0.1875 to 0.1875
- error_memory: float32 [4, 1024, 512], P('dp', 'graph'), may hold values from -6 to 6
- warm_q: float32 [512, 64], replicated, may hold values from -6 to 6
Outputs:
- new_nodes: bfloat16 [4, 4096, 512], P('dp', 'graph')
- update: float32 [1024, 512], P('graph')
- new_error: float32 [4, 1024, 512], P('dp', 'graph')
- new_q: float32 [512, 64], replicated
The draws below stay inside these ranges and needn't reach their ends.
All inputs are finite; a program needn't handle non-finite values.
Results may differ from the reference program's by a relative error of at most 0.0066.
Values may be sent and summed in bfloat16 or wider, within the bound.
No kernel may reach another device: no remote copies, remote signals or barrier semaphores. Data moves between devices by JAX's collectives and lax.ppermute only.
A program may use at most 64 MiB of HBM per device.

```python
import jax
import jax.numpy as jnp
from jax import lax

D = 512
RANK = 64
NODE_DEV = 512
PEER = 8
EDGE_DEV = 2048
NODES = 4096
EDGES = 16384
N_GRAPH = 8
N_DP = 4


def touch_ends(result, rng, least, largest):
    longest = result.shape.index(max(result.shape))
    spots = []
    for shift in (0, 1):
        where = [jax.random.randint(jax.random.fold_in(rng, axis), (), 0, length) for axis, length in enumerate(result.shape)]
        where[longest] = (where[longest] + shift) % result.shape[longest]
        spots.append(tuple(where))
    return result.at[spots[0]].set(least).at[spots[1]].set(largest)


def level_of(key, extent, cuts, smallest, top_value):
    level = 1.0
    for axis_at, blocks in cuts:
        heights = jax.random.uniform(jax.random.fold_in(jax.random.fold_in(key, 6), axis_at), (blocks,), jnp.float32, smallest / len(cuts), top_value / len(cuts))
        level = level * jnp.repeat(jnp.exp(heights), extent[axis_at] // blocks).reshape((-1,) + (1,) * (len(extent) - 1 - axis_at))
    return level


def gaussian(rng, dims, scale, limit, shards=(), held_as=jnp.bfloat16):
    result = scale * jax.random.normal(rng, dims, jnp.float32)
    if shards:
        result = result * level_of(rng, dims, shards, -0.22, 0.18)
    return jnp.clip(result, -limit, limit).astype(held_as)


def setup_inputs(seed: int = 0) -> dict:
    keys = jax.random.split(jax.random.key(seed), 11)
    node_state = gaussian(keys[0], (N_DP, NODES, D), 1.0, 6.0, ((0, 4), (1, 8)))
    edge_state = gaussian(keys[1], (N_DP, EDGES, D), 1.0, 6.0, ((0, 4), (1, 8)))
    senders = touch_ends(jax.random.randint(keys[2], (N_DP, EDGES), 0, NODE_DEV + N_GRAPH * PEER), jax.random.fold_in(keys[2], 1), 0, (NODE_DEV + N_GRAPH * PEER) - 1).astype(jnp.int32)
    receivers = touch_ends(jax.random.randint(keys[3], (N_DP, EDGES), 0, NODE_DEV), jax.random.fold_in(keys[3], 1), 0, NODE_DEV - 1).astype(jnp.int32)
    send_index = touch_ends(jax.random.randint(keys[4], (N_DP, N_GRAPH, N_GRAPH * PEER), 0, NODE_DEV), jax.random.fold_in(keys[4], 1), 0, NODE_DEV - 1).astype(jnp.int32)
    cotangent = gaussian(keys[5], (N_DP, NODES, D), (1.0 / (N_GRAPH * NODE_DEV) ** 0.5), 0.09375, ((0, 4), (1, 8)))
    w_edge = gaussian(keys[6], (3 * D, D), (3 * D) ** -0.5, 0.15625)
    w_node = gaussian(keys[7], (2 * D, D), (2 * D) ** -0.5, 0.1875)
    error_memory = gaussian(keys[8], (N_DP, 2 * D, D), 1.0, 6.0, ((0, 4), (1, 8)), jnp.float32)
    warm_q = gaussian(keys[9], (D, RANK), 1.0, 6.0, (), jnp.float32)
    return dict(node_state=node_state, edge_state=edge_state, senders=senders, receivers=receivers, send_index=send_index, cotangent=cotangent, w_edge=w_edge, w_node=w_node, error_memory=error_memory, warm_q=warm_q)


def silu_slope(pre_act):
    sigmoid_v = jax.nn.sigmoid(pre_act)
    return sigmoid_v * (1.0 + pre_act * (1.0 - sigmoid_v))

def one_group(inputs):
    node_state, edge_state, senders, receivers, send_index, cotangent, w_edge, w_node = inputs
    offsets = (jnp.arange(N_GRAPH, dtype=jnp.int32) * NODE_DEV)[:, None]

    def partition(grad_total, index):
        node_block = lax.dynamic_slice_in_dim(node_state, (index * NODE_DEV).astype(jnp.int32), NODE_DEV, 0)
        cot_block = lax.dynamic_slice_in_dim(cotangent, (index * NODE_DEV).astype(jnp.int32), NODE_DEV, 0)
        edge_block = lax.dynamic_slice_in_dim(edge_state, (index * EDGE_DEV).astype(jnp.int32), EDGE_DEV, 0)
        send_block = lax.dynamic_slice_in_dim(senders, (index * EDGE_DEV).astype(jnp.int32), EDGE_DEV, 0)
        recv_block = lax.dynamic_slice_in_dim(receivers, (index * EDGE_DEV).astype(jnp.int32), EDGE_DEV, 0)
        chosen_rows = lax.dynamic_slice_in_dim(send_index, (index * PEER).astype(jnp.int32), PEER, 1)
        global_rows = (chosen_rows + offsets).reshape(-1)
        halo = node_state[global_rows]
        lookup = jnp.concatenate([node_block, halo], axis=0)
        sender_rows = lookup[send_block]
        receiver_rows = node_block[recv_block]
        joined = jnp.concatenate([edge_block, sender_rows, receiver_rows], axis=1)
        edge_pre = jnp.dot(joined.astype(jnp.float32), w_edge.astype(jnp.float32), preferred_element_type=jnp.float32)
        edge_new = (edge_block.astype(jnp.float32) + jax.nn.silu(edge_pre)).astype(jnp.bfloat16)
        aggregate = jax.ops.segment_sum(edge_new.astype(jnp.float32), recv_block, num_segments=NODE_DEV).astype(jnp.bfloat16)
        node_input = jnp.concatenate([node_block, aggregate], axis=1)
        node_pre = jnp.dot(node_input.astype(jnp.float32), w_node.astype(jnp.float32), preferred_element_type=jnp.float32)
        new_block = (node_block.astype(jnp.float32) + jax.nn.silu(node_pre)).astype(jnp.bfloat16)
        node_delta = (cot_block.astype(jnp.float32) * silu_slope(node_pre)).astype(jnp.bfloat16)
        grad_part = jnp.dot(node_input.T.astype(jnp.float32), node_delta.astype(jnp.float32), preferred_element_type=jnp.float32)
        return (grad_total + grad_part, new_block)
    start = jnp.zeros((2 * D, D), jnp.float32)
    grad_total, blocks = lax.scan(partition, start, jnp.arange(N_GRAPH, dtype=jnp.int32))
    return (blocks.reshape(NODES, D), grad_total)

def reference(node_state, edge_state, senders, receivers, send_index, cotangent, w_edge, w_node, error_memory, warm_q):

    def run_group(inputs):
        return one_group(inputs + (w_edge, w_node))
    new_nodes, gradient = lax.map(run_group, (node_state, edge_state, senders, receivers, send_index, cotangent))
    highest = lax.Precision.HIGHEST
    matrix = gradient + error_memory
    left = jnp.einsum('gij,jr->ir', matrix, warm_q, precision=highest)
    gram = jnp.dot(left.T, left, precision=highest)
    chol = jnp.linalg.cholesky(gram)
    ortho = lax.linalg.triangular_solve(chol, left, left_side=False, lower=True, transpose_a=True)
    new_q = jnp.einsum('gij,ir->jr', matrix, ortho, precision=highest) / N_DP
    update = jnp.dot(ortho, new_q.T, precision=highest)
    new_error = matrix - update[None]
    return (new_nodes, update, new_error, new_q)
```

```python
import functools

import jax
import jax.numpy as jnp
from jax import lax
from jax.experimental import pallas as pl
from jax.experimental.pallas import tpu as pltpu
from jax.sharding import PartitionSpec as P

F32 = jnp.float32
BF16 = jnp.bfloat16
HIGHEST = lax.Precision.HIGHEST
MIB = 1 << 20


def dot_nn(a, b, precision=None):
    return lax.dot_general(
        a, b, (((1,), (0,)), ((), ())), precision=precision, preferred_element_type=F32
    )


def dot_nt(a, b, precision=None):
    return lax.dot_general(
        a, b, (((1,), (1,)), ((), ())), precision=precision, preferred_element_type=F32
    )


def dot_tn(a, b, precision=None):
    return lax.dot_general(
        a, b, (((0,), (0,)), ((), ())), precision=precision, preferred_element_type=F32
    )


def sigmoid(v):
    return 0.5 * jnp.tanh(0.5 * v) + 0.5


def columns_of(row):
    return jnp.broadcast_to(row, (128, row.shape[1])).T


def one_hot_rows(cols, first, width):
    lane = lax.broadcasted_iota(jnp.int32, cols.shape, 1)
    parts = []
    for start in range(0, width, 128):
        size = min(128, width - start)
        hit = jnp.where(cols == lane + (first + start), 1.0, 0.0).astype(BF16)
        parts.append(hit[:, :size])
    return parts[0] if len(parts) == 1 else jnp.concatenate(parts, axis=1)


def pick_kernel(index_ref, node_ref, out_ref):
    nodes = node_ref.shape[0]
    count = index_ref.shape[1]
    row = lax.broadcasted_iota(jnp.int32, (nodes, count), 0)
    hit = jnp.where(row == index_ref[...], 1.0, 0.0).astype(BF16)
    out_ref[...] = dot_tn(hit, node_ref[...]).astype(BF16)


def edge_kernel(edge_ref, send_ref, recv_ref, node_ref, weight_ref, out_ref, table):
    nodes, features = node_ref.shape

    @pl.when(pl.program_id(0) == 0)
    def _():
        node = node_ref[...]
        table[0:features, :] = weight_ref[0:features, :]
        own = dot_nn(node, weight_ref[features : 2 * features, :])
        table[features : features + nodes, :] = own.astype(BF16)
        into = dot_nn(node, weight_ref[2 * features : 3 * features, :])
        table[features + nodes :, :] = into.astype(BF16)

    left = jnp.concatenate(
        [
            edge_ref[...],
            one_hot_rows(columns_of(send_ref[...]), 0, nodes),
            one_hot_rows(columns_of(recv_ref[...]), 0, nodes),
        ],
        axis=1,
    )
    out_ref[...] = dot_nn(left, table[...])


def node_kernel(
    pre_ref,
    edge_ref,
    send_ref,
    recv_ref,
    halo_ref,
    weight_ref,
    node_ref,
    cot_ref,
    wnode_ref,
    new_ref,
    grad_ref,
    table,
    total,
):
    nodes = node_ref.shape[0]
    halo = halo_ref.shape[0]

    @pl.when(pl.program_id(0) == 0)
    def _():
        table[...] = dot_nn(halo_ref[...], weight_ref[...]).astype(BF16)
        total[...] = jnp.zeros_like(total)

    hot = one_hot_rows(columns_of(send_ref[...]), nodes, halo)
    pre = pre_ref[...] + dot_nn(hot, table[...])
    edge_new = (edge_ref[...].astype(F32) + pre * sigmoid(pre)).astype(BF16)
    row = lax.broadcasted_iota(jnp.int32, (nodes, recv_ref.shape[1]), 0)
    incidence = jnp.where(row == recv_ref[...], 1.0, 0.0).astype(BF16)
    total[...] += dot_nn(incidence, edge_new)

    @pl.when(pl.program_id(0) == pl.num_programs(0) - 1)
    def _():
        node = node_ref[...]
        joined = jnp.concatenate([node, total[...].astype(BF16)], axis=1)
        node_pre = dot_nn(joined, wnode_ref[...])
        gate = sigmoid(node_pre)
        new_ref[...] = (node.astype(F32) + node_pre * gate).astype(BF16)
        delta = cot_ref[...].astype(F32) * (gate * (1.0 + node_pre * (1.0 - gate)))
        grad_ref[...] = dot_tn(joined, delta.astype(BF16)).astype(BF16)


def matrix_kernel(got_ref, error_ref, warm_ref, matrix_ref, left_ref):
    matrix = error_ref[...]
    for part in range(got_ref.shape[0]):
        matrix = matrix + got_ref[part].astype(F32)
    matrix_ref[...] = matrix
    left_ref[...] = dot_nt(warm_ref[...], matrix, HIGHEST)


def right_kernel(left_ref, matrix_ref, right_ref):
    right_ref[...] = dot_nn(left_ref[...], matrix_ref[...], HIGHEST)


def inverse_factor(gram, group=8):
    rank = gram.shape[0]
    row = lax.broadcasted_iota(jnp.int32, (rank, rank), 0)
    col = lax.broadcasted_iota(jnp.int32, (rank, rank), 1)
    work = jnp.concatenate([gram, jnp.where(row == col, 1.0, 0.0)], axis=1)
    wide = work.shape[1]
    row = lax.broadcasted_iota(jnp.int32, (rank, wide), 0)
    scale = jnp.ones((rank, wide), F32)
    for start in range(0, rank, group):
        cols = [
            jnp.broadcast_to(work[:, start + j : start + j + 1], (rank, wide))
            for j in range(group)
        ]
        for j in range(group):
            k = start + j
            pivot = jnp.broadcast_to(cols[j][k : k + 1, :], (rank, wide))
            factor = jnp.where(row > k, cols[j] / pivot, 0.0)
            scale = jnp.where(row == k, lax.rsqrt(pivot), scale)
            work = work - factor * work[k : k + 1, :]
            for i in range(j + 1, group):
                cols[i] = cols[i] - factor * cols[i][k : k + 1, :]
    return (work * scale)[:, rank:]


def final_kernel(right_ref, left_ref, matrix_ref, warm_ref, q_ref, update_ref, error_ref, *, groups):
    right = right_ref[...]
    gram = dot_nt(right, warm_ref[...], HIGHEST)
    inverse = inverse_factor(gram)
    ortho = dot_nn(inverse, left_ref[...], HIGHEST)
    new_q = dot_nn(inverse, right, HIGHEST) / groups
    update = dot_tn(ortho, new_q, HIGHEST)
    q_ref[...] = new_q
    update_ref[...] = update
    error_ref[...] = matrix_ref[...] - update


def exchange(x, axes, size, mask):
    return lax.ppermute(x, axes, [(i, i ^ mask) for i in range(size)])


def body(
    node_state,
    edge_state,
    senders,
    receivers,
    send_index,
    cotangent,
    w_edge,
    w_node,
    error_memory,
    warm_q,
):
    node_block = node_state[0]
    edge_block = edge_state[0]
    nodes, features = node_block.shape
    edges = edge_block.shape[0]
    partitions = lax.axis_size("graph")
    replicas = lax.axis_size("dp")
    rank = warm_q.shape[1]
    warm = warm_q.T
    tile = 256
    steps = edges // tile
    params = functools.partial(pltpu.CompilerParams, vmem_limit_bytes=32 * MIB)

    outgoing = pl.pallas_call(
        pick_kernel,
        out_shape=jax.ShapeDtypeStruct((send_index.shape[2], features), BF16),
        compiler_params=params(),
    )(send_index[0], node_block)
    incoming = lax.all_to_all(
        outgoing.reshape(partitions, -1, features), "graph", split_axis=0, concat_axis=0, tiled=True
    ).reshape(-1, features)

    whole = lambda shape: pl.BlockSpec(shape, lambda i: (0,) * len(shape))
    edge_pre = pl.pallas_call(
        edge_kernel,
        grid=(steps,),
        in_specs=[
            pl.BlockSpec((tile, features), lambda i: (i, 0)),
            pl.BlockSpec((1, tile), lambda i: (0, i)),
            pl.BlockSpec((1, tile), lambda i: (0, i)),
            whole(node_block.shape),
            whole(w_edge.shape),
        ],
        out_specs=pl.BlockSpec((tile, features), lambda i: (i, 0)),
        out_shape=jax.ShapeDtypeStruct((edges, features), F32),
        scratch_shapes=[pltpu.VMEM((features + 2 * nodes, features), BF16)],
        compiler_params=params(),
    )(edge_block, senders, receivers, node_block, w_edge)

    new_block, gradient = pl.pallas_call(
        node_kernel,
        grid=(steps,),
        in_specs=[
            pl.BlockSpec((tile, features), lambda i: (i, 0)),
            pl.BlockSpec((tile, features), lambda i: (i, 0)),
            pl.BlockSpec((1, tile), lambda i: (0, i)),
            pl.BlockSpec((1, tile), lambda i: (0, i)),
            whole(incoming.shape),
            pl.BlockSpec((features, features), lambda i: (1, 0)),
            whole(node_block.shape),
            whole(node_block.shape),
            whole(w_node.shape),
        ],
        out_specs=[whole(node_block.shape), whole(w_node.shape)],
        out_shape=[
            jax.ShapeDtypeStruct(node_block.shape, BF16),
            jax.ShapeDtypeStruct(w_node.shape, BF16),
        ],
        scratch_shapes=[
            pltpu.VMEM(incoming.shape, BF16),
            pltpu.VMEM((nodes, features), F32),
        ],
        compiler_params=params(),
    )(
        edge_pre,
        edge_block,
        senders,
        receivers,
        incoming,
        w_edge,
        node_block,
        cotangent[0],
        w_node,
    )

    rows = w_node.shape[0] // partitions
    got = lax.all_to_all(
        gradient.reshape(partitions, rows, features),
        "graph",
        split_axis=0,
        concat_axis=0,
        tiled=True,
    )
    matrix, left = pl.pallas_call(
        matrix_kernel,
        out_shape=[
            jax.ShapeDtypeStruct((rows, features), F32),
            jax.ShapeDtypeStruct((rank, rows), F32),
        ],
        compiler_params=params(),
    )(got, error_memory[0], warm)
    mask = 1
    while mask < replicas:
        left = left + exchange(left, "dp", replicas, mask)
        mask *= 2

    right = pl.pallas_call(
        right_kernel,
        out_shape=jax.ShapeDtypeStruct((rank, features), F32),
        compiler_params=params(),
    )(left, matrix)
    side = lax.axis_index("dp") % 2
    half = rank // 2
    low, high = right[:half], right[half:]
    kept = jnp.where(side == 0, low, high)
    given = jnp.where(side == 0, high, low)
    kept = kept + exchange(given, "dp", replicas, 1)
    mask = 2
    while mask < replicas:
        kept = kept + exchange(kept, "dp", replicas, mask)
        mask *= 2
    mask = 1
    while mask < partitions:
        kept = kept + exchange(kept, "graph", partitions, mask)
        mask *= 2
    other = exchange(kept, "dp", replicas, 1)
    right = jnp.concatenate(
        [jnp.where(side == 0, kept, other), jnp.where(side == 0, other, kept)], axis=0
    )

    new_q, update, new_error = pl.pallas_call(
        functools.partial(final_kernel, groups=replicas),
        out_shape=[
            jax.ShapeDtypeStruct((rank, features), F32),
            jax.ShapeDtypeStruct((rows, features), F32),
            jax.ShapeDtypeStruct((rows, features), F32),
        ],
        compiler_params=params(),
    )(right, left, matrix, warm)
    return (new_block[None], update, new_error[None], new_q.T)


def solution(mesh):
    return jax.shard_map(
        body,
        mesh=mesh,
        in_specs=(
            P("dp", "graph", None),
            P("dp", "graph", None),
            P("dp", "graph"),
            P("dp", "graph"),
            P("dp", "graph", None),
            P("dp", "graph", None),
            P(),
            P(),
            P("dp", "graph", None),
            P(),
        ),
        out_specs=(P("dp", "graph", None), P("graph", None), P("dp", "graph", None), P()),
        check_vma=False,
    )
```

```python
import functools

import jax
import jax.numpy as jnp
from jax import lax
from jax.experimental import pallas as pl
from jax.experimental.pallas import tpu as pltpu
from jax.sharding import PartitionSpec as P

F32 = jnp.float32
BF16 = jnp.bfloat16
HIGHEST = lax.Precision.HIGHEST
MIB = 1 << 20


def dot_nn(a, b, precision=None):
    return lax.dot_general(
        a, b, (((1,), (0,)), ((), ())), precision=precision, preferred_element_type=F32
    )


def dot_nt(a, b, precision=None):
    return lax.dot_general(
        a, b, (((1,), (1,)), ((), ())), precision=precision, preferred_element_type=F32
    )


def dot_tn(a, b, precision=None):
    return lax.dot_general(
        a, b, (((0,), (0,)), ((), ())), precision=precision, preferred_element_type=F32
    )


def sigmoid(v):
    return 0.5 * jnp.tanh(0.5 * v) + 0.5


def columns_of(row):
    return jnp.broadcast_to(row, (128, row.shape[1])).T


def one_hot_rows(cols, first, width):
    lane = lax.broadcasted_iota(jnp.int32, cols.shape, 1)
    parts = []
    for start in range(0, width, 128):
        size = min(128, width - start)
        hit = jnp.where(cols == lane + (first + start), 1.0, 0.0).astype(BF16)
        parts.append(hit[:, :size])
    return parts[0] if len(parts) == 1 else jnp.concatenate(parts, axis=1)


def pick_kernel(index_hbm, node_hbm, out_ref, index, node, sems):
    copies = [
        pltpu.make_async_copy(index_hbm, index, sems.at[0]),
        pltpu.make_async_copy(node_hbm, node, sems.at[1]),
    ]
    for copy in copies:
        copy.start()
    for copy in copies:
        copy.wait()
    row = lax.broadcasted_iota(jnp.int32, (node.shape[0], index.shape[1]), 0)
    hit = jnp.where(row == index[...], 1.0, 0.0).astype(BF16)
    out_ref[...] = dot_tn(hit, node[...]).astype(BF16)


def layer_kernel(
    place_ref,
    send_ref,
    recv_ref,
    halo_ref,
    edge_hbm,
    node_hbm,
    cot_hbm,
    wedge_hbm,
    wnode_hbm,
    new_ref,
    near_send_ref,
    near_keep_ref,
    far_send_ref,
    far_keep_ref,
    grad,
    edge,
    look,
    weight,
    table,
    total,
    cot,
    joined,
    wnode,
    sems,
    edge_sems,
    *,
    tile,
):
    nodes, features = node_hbm.shape
    halo = halo_ref.shape[0]
    edges = edge_hbm.shape[0]
    steps = edges // tile
    reach = nodes + halo

    def edge_copy(step):
        rows = pl.ds(step * tile, tile)
        return pltpu.make_async_copy(edge_hbm.at[rows, :], edge.at[rows, :], edge_sems.at[step])

    node_copy = pltpu.make_async_copy(node_hbm, look.at[pl.ds(0, nodes), :], sems.at[0])
    weight_copies = [
        pltpu.make_async_copy(
            wedge_hbm.at[pl.ds(part * features, features), :],
            weight.at[pl.ds(part * features, features), :],
            sems.at[1 + part],
        )
        for part in (1, 2, 0)
    ]
    last = [
        pltpu.make_async_copy(wnode_hbm, wnode, sems.at[4]),
        pltpu.make_async_copy(cot_hbm, cot, sems.at[5]),
    ]
    node_copy.start()
    for copy in weight_copies:
        copy.start()
    for step in range(steps):
        edge_copy(step).start()
    for copy in last:
        copy.start()
    look[nodes:, :] = halo_ref[...]
    node_copy.wait()
    joined[:, 0:features] = look[0:nodes, :]
    weight_copies[0].wait()
    own = dot_nn(look[...], weight[features : 2 * features, :])
    table[features : features + reach, :] = (0.5 * own).astype(BF16)
    weight_copies[1].wait()
    into = dot_nn(look[0:nodes, :], weight[2 * features :, :])
    table[features + reach :, :] = (0.5 * into).astype(BF16)
    weight_copies[2].wait()
    table[0:features, :] = weight[0:features, :] * 0.5

    for step in range(steps):
        rows = pl.ds(step * tile, tile)
        edge_copy(step).wait()
        block = edge[rows, :]
        recv = recv_ref[:, rows]
        left = jnp.concatenate(
            [
                block,
                one_hot_rows(columns_of(send_ref[:, rows]), 0, reach),
                one_hot_rows(columns_of(recv), 0, nodes),
            ],
            axis=1,
        )
        half = dot_nn(left, table[...])
        edge_new = (block.astype(F32) + (half + half * jnp.tanh(half))).astype(BF16)
        row = lax.broadcasted_iota(jnp.int32, (nodes, tile), 0)
        incidence = jnp.where(row == recv, 1.0, 0.0).astype(BF16)
        part = dot_nn(incidence, edge_new)
        if step == 0:
            total[...] = part
        else:
            total[...] += part

    joined[:, features:] = total[...].astype(BF16)
    for copy in last:
        copy.wait()
    block = 128
    for step in range(nodes // block):
        rows = pl.ds(step * block, block)
        half = 0.5 * dot_nn(joined[rows, :], wnode[...])
        turn = jnp.tanh(half)
        node = joined[rows, 0:features].astype(F32)
        new_ref[rows, :] = (node + (half + half * turn)).astype(BF16)
        slope = (0.5 + 0.5 * turn) * (1.0 + half * (1.0 - turn))
        look[rows, :] = (cot[rows, :].astype(F32) * slope).astype(BF16)
    grad[...] = dot_tn(joined[...], look[0:nodes, :])
    me = place_ref[0]
    side = place_ref[1]
    parts, size, width = near_keep_ref.shape
    bits = (2 * parts).bit_length() - 1
    for refs, order, turn in (
        ((near_keep_ref, near_send_ref), stage_order(bits, False), side),
        ((far_keep_ref, far_send_ref), stage_order(bits, True), 1 - side),
    ):
        column = pl.multiple_of(turn * width, width)
        for slot in range(2 * parts):
            offset = 0
            for stage, bit in enumerate(order):
                offset |= ((slot >> (bits - 1 - stage)) & 1) << bit
            row = pl.multiple_of((me ^ offset) * size, size)
            block = grad[pl.ds(row, size), pl.ds(column, width)]
            ref = refs[slot // parts]
            ref[slot % parts] = block.astype(ref.dtype)


def matrix_kernel(place_ref, keep_ref, got_ref, error_ref, near_ref, far_ref):
    width = near_ref.shape[1]
    for half, (out_ref, turn) in enumerate(
        ((near_ref, place_ref[1]), (far_ref, 1 - place_ref[1]))
    ):
        column = pl.multiple_of(turn * width, width)
        out_ref[...] = (
            keep_ref[half, 0] + got_ref[half, 0].astype(F32) + error_ref[:, pl.ds(column, width)]
        )


def left_kernel(place_ref, mean_ref, got_ref, warm_ref, sum_ref, left_ref):
    width = mean_ref.shape[1]
    total = mean_ref[...] + got_ref[...].astype(F32)
    sum_ref[...] = total
    column = pl.multiple_of(place_ref[1] * width, width)
    left_ref[...] = dot_nt(warm_ref[:, pl.ds(column, width)], total, HIGHEST)


def right_kernel(left_ref, other_ref, sum_ref, full_ref, right_ref):
    left = left_ref[...] + other_ref[...]
    full_ref[...] = left
    right_ref[...] = dot_nn(left, sum_ref[...], HIGHEST)


def inverse_factor(gram, group=8):
    rank = gram.shape[0]
    row = lax.broadcasted_iota(jnp.int32, (rank, rank), 0)
    col = lax.broadcasted_iota(jnp.int32, (rank, rank), 1)
    work = jnp.concatenate([gram, jnp.where(row == col, 1.0, 0.0)], axis=1)
    wide = work.shape[1]
    row = lax.broadcasted_iota(jnp.int32, (rank, wide), 0)
    scale = jnp.ones((rank, wide), F32)
    for start in range(0, rank, group):
        cols = [
            jnp.broadcast_to(work[:, start + j : start + j + 1], (rank, wide))
            for j in range(group)
        ]
        for j in range(group):
            k = start + j
            pivot = jnp.broadcast_to(cols[j][k : k + 1, :], (rank, wide))
            factor = jnp.where(row > k, cols[j] / pivot, 0.0)
            scale = jnp.where(row == k, lax.rsqrt(pivot), scale)
            work = work - factor * work[k : k + 1, :]
            for i in range(j + 1, group):
                cols[i] = cols[i] - factor * cols[i][k : k + 1, :]
    return (work * scale)[:, rank:]


def final_kernel(
    place_ref, near_ref, far_ref, left_ref, near_matrix_ref, far_matrix_ref, warm_ref, q_ref, update_ref, error_ref, *, groups
):
    width = near_ref.shape[1]
    near = pl.ds(pl.multiple_of(place_ref[1] * width, width), width)
    far = pl.ds(pl.multiple_of((1 - place_ref[1]) * width, width), width)
    gram = dot_nt(near_ref[...], warm_ref[:, near], HIGHEST) + dot_nt(
        far_ref[...], warm_ref[:, far], HIGHEST
    )
    inverse = inverse_factor(gram)
    ortho = dot_nn(inverse, left_ref[...], HIGHEST)
    for columns, right_ref, matrix_ref in (
        (near, near_ref, near_matrix_ref),
        (far, far_ref, far_matrix_ref),
    ):
        new_q = dot_nn(inverse, right_ref[...], HIGHEST) / groups
        update = dot_tn(ortho, new_q, HIGHEST)
        q_ref[:, columns] = new_q
        update_ref[:, columns] = update
        error_ref[:, columns] = matrix_ref[...] - update


def stage_order(bits, swapped):
    order = list(range(bits))
    if swapped and bits > 1:
        order[0], order[1] = 1, 0
    return order


def exchange(x, axes, size, mask):
    return lax.ppermute(x, axes, [(i, i ^ mask) for i in range(size)])


def body(
    node_state,
    edge_state,
    senders,
    receivers,
    send_index,
    cotangent,
    w_edge,
    w_node,
    error_memory,
    warm_q,
):
    node_block = node_state[0]
    edge_block = edge_state[0]
    nodes, features = node_block.shape
    edges = edge_block.shape[0]
    partitions = lax.axis_size("graph")
    replicas = lax.axis_size("dp")
    rank = warm_q.shape[1]
    warm = warm_q.T
    tile = 512
    params = functools.partial(pltpu.CompilerParams, vmem_limit_bytes=24 * MIB)

    vmem = pl.BlockSpec(memory_space=pltpu.VMEM)
    hbm = pl.BlockSpec(memory_space=pltpu.HBM)
    outgoing = pl.pallas_call(
        pick_kernel,
        in_specs=[hbm] * 2,
        out_specs=vmem,
        out_shape=jax.ShapeDtypeStruct((send_index.shape[2], features), BF16),
        scratch_shapes=[
            pltpu.VMEM((1, send_index.shape[2]), jnp.int32),
            pltpu.VMEM(node_block.shape, BF16),
            pltpu.SemaphoreType.DMA((2,)),
        ],
        compiler_params=pltpu.CompilerParams(vmem_limit_bytes=60 * MIB),
    )(send_index[0], node_block)
    incoming = lax.all_to_all(
        outgoing.reshape(partitions, -1, features), "graph", split_axis=0, concat_axis=0, tiled=True
    ).reshape(-1, features)

    reach = nodes + incoming.shape[0]
    rows = w_node.shape[0] // partitions
    width = features // 2
    place = jnp.stack([lax.axis_index("graph"), lax.axis_index("dp") % 2]).astype(jnp.int32)
    smem = pl.BlockSpec(memory_space=pltpu.SMEM)
    piece = (partitions // 2, rows, width)
    new_block, near_send, near_keep, far_send, far_keep = pl.pallas_call(
        functools.partial(layer_kernel, tile=tile),
        in_specs=[smem] + [vmem] * 3 + [hbm] * 5,
        out_specs=[vmem] * 5,
        out_shape=[
            jax.ShapeDtypeStruct(node_block.shape, BF16),
            jax.ShapeDtypeStruct(piece, BF16),
            jax.ShapeDtypeStruct(piece, F32),
            jax.ShapeDtypeStruct(piece, BF16),
            jax.ShapeDtypeStruct(piece, F32),
        ],
        scratch_shapes=[
            pltpu.VMEM(w_node.shape, F32),
            pltpu.VMEM((edges, features), BF16),
            pltpu.VMEM((reach, features), BF16),
            pltpu.VMEM(w_edge.shape, BF16),
            pltpu.VMEM((features + reach + nodes, features), BF16),
            pltpu.VMEM((nodes, features), F32),
            pltpu.VMEM((nodes, features), BF16),
            pltpu.VMEM((nodes, w_node.shape[0]), BF16),
            pltpu.VMEM(w_node.shape, BF16),
            pltpu.SemaphoreType.DMA((6,)),
            pltpu.SemaphoreType.DMA((edges // tile,)),
        ],
        compiler_params=pltpu.CompilerParams(vmem_limit_bytes=60 * MIB),
    )(
        place,
        senders,
        receivers,
        incoming,
        edge_block,
        node_block,
        cotangent[0],
        w_edge,
        w_node,
    )

    bits = partitions.bit_length() - 1
    near_order, far_order = stage_order(bits, False), stage_order(bits, True)

    def swap(x, bit):
        return exchange(x, "graph", partitions, 1 << bit)

    def halve(keep, got):
        total = keep + got.astype(F32)
        count = total.shape[-3] // 2
        return total[..., :count, :, :], total[..., count:, :, :].astype(BF16)

    near_got = swap(near_send, near_order[0])
    far_got = swap(far_send, far_order[0])
    near_keep, near_send = halve(near_keep, near_got)
    far_keep, far_send = halve(far_keep, far_got)
    near_got = swap(near_send, near_order[1])
    far_got = swap(far_send, far_order[1])
    keep = jnp.stack([near_keep, far_keep])
    got = jnp.stack([near_got, far_got])
    for bit in near_order[2:]:
        keep, send = halve(keep, got)
        got = swap(send, bit)

    near_matrix, far_matrix = pl.pallas_call(
        matrix_kernel,
        in_specs=[smem] + [vmem] * 3,
        out_shape=[jax.ShapeDtypeStruct((rows, width), F32)] * 2,
        compiler_params=params(),
    )(place, keep, got, error_memory[0])
    mean = near_matrix + exchange(far_matrix, "dp", replicas, 1)
    mask = 2
    while 2 * mask < replicas:
        mean = mean + exchange(mean, "dp", replicas, mask)
        mask *= 2
    got = exchange(mean, "dp", replicas, mask)
    total, left = pl.pallas_call(
        left_kernel,
        in_specs=[smem] + [vmem] * 3,
        out_shape=[
            jax.ShapeDtypeStruct((rows, width), F32),
            jax.ShapeDtypeStruct((rank, rows), F32),
        ],
        compiler_params=params(),
    )(place, mean, got, warm)
    other = exchange(left, "dp", replicas, 1)
    left, right = pl.pallas_call(
        right_kernel,
        out_shape=[
            jax.ShapeDtypeStruct((rank, rows), F32),
            jax.ShapeDtypeStruct((rank, width), F32),
        ],
        compiler_params=params(),
    )(left, other, total)
    for bit in range(bits):
        right = right + swap(right, bit)
    far_right = exchange(right, "dp", replicas, 1)

    new_q, update, new_error = pl.pallas_call(
        functools.partial(final_kernel, groups=replicas),
        in_specs=[smem] + [vmem] * 6,
        out_shape=[
            jax.ShapeDtypeStruct((rank, features), F32),
            jax.ShapeDtypeStruct((rows, features), F32),
            jax.ShapeDtypeStruct((rows, features), F32),
        ],
        compiler_params=params(),
    )(place, right, far_right, left, near_matrix, far_matrix, warm)
    return (new_block[None], update, new_error[None], new_q.T)


def solution(mesh):
    return jax.shard_map(
        body,
        mesh=mesh,
        in_specs=(
            P("dp", "graph", None),
            P("dp", "graph", None),
            P("dp", "graph"),
            P("dp", "graph"),
            P("dp", "graph", None),
            P("dp", "graph", None),
            P(),
            P(),
            P("dp", "graph", None),
            P(),
        ),
        out_specs=(P("dp", "graph", None), P("graph", None), P("dp", "graph", None), P()),
        check_vma=False,
    )
```

```python
import functools

import jax
import jax.numpy as jnp
from jax import lax
from jax.experimental import pallas as pl
from jax.experimental.pallas import tpu as pltpu
from jax.sharding import PartitionSpec as P

F32 = jnp.float32
BF16 = jnp.bfloat16
HIGHEST = lax.Precision.HIGHEST
MIB = 1 << 20


def dot_nn(a, b, precision=None):
    return lax.dot_general(
        a, b, (((1,), (0,)), ((), ())), precision=precision, preferred_element_type=F32
    )


def dot_nt(a, b, precision=None):
    return lax.dot_general(
        a, b, (((1,), (1,)), ((), ())), precision=precision, preferred_element_type=F32
    )


def dot_tn(a, b, precision=None):
    return lax.dot_general(
        a, b, (((0,), (0,)), ((), ())), precision=precision, preferred_element_type=F32
    )


def sigmoid(v):
    return 0.5 * jnp.tanh(0.5 * v) + 0.5


def columns_of(row):
    return jnp.broadcast_to(row, (128, row.shape[1])).T


def hits(a, b):
    return jnp.where(a == b, jnp.ones((), BF16), jnp.zeros((), BF16))


def one_hot_rows(cols, first, width):
    cols = cols.astype(jnp.int16)
    lane = lax.broadcasted_iota(jnp.int32, cols.shape, 1)
    parts = []
    for start in range(0, width, 128):
        size = min(128, width - start)
        parts.append(hits(cols, (lane + (first + start)).astype(jnp.int16))[:, :size])
    return parts[0] if len(parts) == 1 else jnp.concatenate(parts, axis=1)


def one_hot_columns(row, height):
    index = lax.broadcasted_iota(jnp.int32, (height, row.shape[1]), 0).astype(jnp.int16)
    return hits(index, jnp.broadcast_to(row, index.shape).astype(jnp.int16))


def pick_kernel(index_hbm, node_hbm, out_ref, index, node, sems):
    copies = [
        pltpu.make_async_copy(index_hbm, index, sems.at[0]),
        pltpu.make_async_copy(node_hbm, node, sems.at[1]),
    ]
    for copy in copies:
        copy.start()
    for copy in copies:
        copy.wait()
    hit = one_hot_columns(index[...], node.shape[0])
    out_ref[...] = dot_tn(hit, node[...]).astype(BF16)


def edge_kernel(
    send_hbm, recv_hbm, edge_hbm, node_hbm, wedge_hbm, pre_hbm, send, recv, edge, node, weight, table, pre, sems, edge_sems, pre_sems, *, tile
):
    nodes, features = node_hbm.shape
    steps = edge_hbm.shape[0] // tile

    def edge_copy(step):
        rows = pl.ds(step * tile, tile)
        return pltpu.make_async_copy(edge_hbm.at[rows, :], edge.at[rows, :], edge_sems.at[step])

    def pre_copy(step):
        rows = pl.ds(step * tile, tile)
        return pltpu.make_async_copy(pre.at[rows, :], pre_hbm.at[rows, :], pre_sems.at[step])

    node_copy = pltpu.make_async_copy(node_hbm, node, sems.at[0])
    weight_copies = [
        pltpu.make_async_copy(
            wedge_hbm.at[pl.ds(part * features, features), :],
            weight.at[pl.ds(part * features, features), :],
            sems.at[1 + part],
        )
        for part in (1, 2, 0)
    ]
    index_copies = [
        pltpu.make_async_copy(send_hbm, send, sems.at[4]),
        pltpu.make_async_copy(recv_hbm, recv, sems.at[5]),
    ]
    node_copy.start()
    for copy in weight_copies + index_copies:
        copy.start()
    for step in range(steps):
        edge_copy(step).start()
    node_copy.wait()
    weight_copies[0].wait()
    own = dot_nn(node[...], weight[features : 2 * features, :])
    table[features : features + nodes, :] = (0.5 * own).astype(BF16)
    weight_copies[1].wait()
    into = dot_nn(node[...], weight[2 * features :, :])
    table[features + nodes :, :] = (0.5 * into).astype(BF16)
    weight_copies[2].wait()
    table[0:features, :] = weight[0:features, :] * 0.5
    for copy in index_copies:
        copy.wait()
    for step in range(steps):
        rows = pl.ds(step * tile, tile)
        edge_copy(step).wait()
        left = jnp.concatenate(
            [
                edge[rows, :],
                one_hot_rows(columns_of(send[:, rows]), 0, nodes),
                one_hot_rows(columns_of(recv[:, rows]), 0, nodes),
            ],
            axis=1,
        )
        pre[rows, :] = dot_nn(left, table[...]).astype(pre.dtype)
        pre_copy(step).start()
    for step in range(steps):
        pre_copy(step).wait()


def node_kernel(
    send_ref,
    recv_ref,
    halo_ref,
    node_ref,
    cot_ref,
    wnode_ref,
    pre_hbm,
    edge_hbm,
    wedge_hbm,
    new_ref,
    near_send_ref,
    near_keep_ref,
    far_send_ref,
    far_keep_ref,
    pre,
    edge,
    weight,
    table,
    total,
    gathered,
    delta,
    grad,
    sems,
    edge_sems,
    pre_sems,
    *,
    tile,
):
    nodes, features = node_ref.shape
    steps = edge_hbm.shape[0] // tile

    def edge_copy(step):
        rows = pl.ds(step * tile, tile)
        return pltpu.make_async_copy(edge_hbm.at[rows, :], edge.at[rows, :], edge_sems.at[step])

    def pre_copy(step):
        rows = pl.ds(step * tile, tile)
        return pltpu.make_async_copy(pre_hbm.at[rows, :], pre.at[rows, :], pre_sems.at[step])

    weight_copy = pltpu.make_async_copy(
        wedge_hbm.at[pl.ds(features, features), :], weight, sems.at[0]
    )
    weight_copy.start()
    for step in range(steps):
        pre_copy(step).start()
        edge_copy(step).start()
    weight_copy.wait()
    table[...] = (0.5 * dot_nn(halo_ref[...], weight[...])).astype(BF16)
    for step in range(steps):
        rows = pl.ds(step * tile, tile)
        hot = one_hot_rows(columns_of(send_ref[:, rows]), nodes, halo_ref.shape[0])
        incidence = one_hot_columns(recv_ref[:, rows], nodes)
        pre_copy(step).wait()
        edge_copy(step).wait()
        half = pre[rows, :].astype(F32) + dot_nn(hot, table[...])
        edge_new = (edge[rows, :].astype(F32) + (half + half * jnp.tanh(half))).astype(BF16)
        part = dot_nn(incidence, edge_new)
        if step == 0:
            total[...] = part
        else:
            total[...] += part

    gathered[...] = total[...].astype(BF16)
    block = 128
    for step in range(nodes // block):
        rows = pl.ds(step * block, block)
        node = node_ref[rows, :]
        joined = jnp.concatenate([node, gathered[rows, :]], axis=1)
        half = 0.5 * dot_nn(joined, wnode_ref[...])
        turn = jnp.tanh(half)
        new_ref[rows, :] = (node.astype(F32) + (half + half * turn)).astype(BF16)
        slope = (0.5 + 0.5 * turn) * (1.0 + half * (1.0 - turn))
        delta[rows, :] = (cot_ref[rows, :].astype(F32) * slope).astype(BF16)
    grad[0:features, :] = dot_tn(node_ref[...], delta[...])
    grad[features:, :] = dot_tn(gathered[...], delta[...])
    me = lax.axis_index("graph")
    side = lax.axis_index("dp") % 2
    parts, size, width = near_keep_ref.shape
    bits = (2 * parts).bit_length() - 1
    for refs, order, turn in (
        ((near_keep_ref, near_send_ref), stage_order(bits, False), side),
        ((far_keep_ref, far_send_ref), stage_order(bits, True), 1 - side),
    ):
        column = pl.multiple_of(turn * width, width)
        for slot in range(2 * parts):
            offset = 0
            for stage, bit in enumerate(order):
                offset |= ((slot >> (bits - 1 - stage)) & 1) << bit
            row = pl.multiple_of((me ^ offset) * size, size)
            block = grad[pl.ds(row, size), pl.ds(column, width)]
            ref = refs[slot // parts]
            ref[slot % parts] = block.astype(ref.dtype)


def matrix_kernel(keep_ref, got_ref, error_ref, near_ref, far_ref):
    width = near_ref.shape[1]
    side = lax.axis_index("dp") % 2
    for half, (out_ref, turn) in enumerate(((near_ref, side), (far_ref, 1 - side))):
        column = pl.multiple_of(turn * width, width)
        out_ref[...] = (
            keep_ref[half, 0] + got_ref[half, 0].astype(F32) + error_ref[:, pl.ds(column, width)]
        )


def left_kernel(mean_ref, got_ref, warm_ref, sum_ref, left_ref):
    width = mean_ref.shape[1]
    total = mean_ref[...].astype(F32) + got_ref[...].astype(F32)
    sum_ref[...] = total
    column = pl.multiple_of((lax.axis_index("dp") % 2) * width, width)
    left_ref[...] = dot_nt(warm_ref[:, pl.ds(column, width)], total, HIGHEST)


def right_kernel(left_ref, other_ref, sum_ref, full_ref, right_ref):
    left = left_ref[...] + other_ref[...]
    full_ref[...] = left
    right_ref[...] = dot_nn(left, sum_ref[...], HIGHEST)


def inverse_factor(gram, group=8):
    rank = gram.shape[0]
    row = lax.broadcasted_iota(jnp.int32, (rank, rank), 0)
    col = lax.broadcasted_iota(jnp.int32, (rank, rank), 1)
    joined = jnp.concatenate([gram, jnp.where(row == col, 1.0, 0.0)], axis=1)
    wide = joined.shape[1]
    row = lax.broadcasted_iota(jnp.int32, (group, wide), 0)
    work = [joined[start : start + group] for start in range(0, rank, group)]
    for g in range(rank // group):
        cols = [
            {
                b: jnp.broadcast_to(work[b][:, k : k + 1], (group, wide))
                for b in range(g, rank // group)
            }
            for k in range(g * group, (g + 1) * group)
        ]
        scale = jnp.ones((group, wide), F32)
        for j in range(group):
            pivot = cols[j][g][j : j + 1]
            scale = jnp.where(row == j, lax.rsqrt(pivot), scale)
            inverse = 1.0 / pivot
            source = work[g][j : j + 1]
            sources = [cols[i][g][j : j + 1] for i in range(j + 1, group)]
            for b in range(g, rank // group):
                if b == g and j == group - 1:
                    continue
                factor = cols[j][b] * inverse
                if b == g:
                    factor = jnp.where(row > j, factor, 0.0)
                work[b] = work[b] - factor * source
                for i in range(j + 1, group):
                    cols[i][b] = cols[i][b] - factor * sources[i - j - 1]
        work[g] = work[g] * scale
    return jnp.concatenate(work, axis=0)[:, rank:]


def split3(a):
    high = a.astype(BF16)
    return high, (a - high.astype(F32)).astype(BF16)


def dot3_nn(a, b):
    a_high, a_low = split3(a)
    b_high, b_low = split3(b)
    return dot_nn(
        jnp.concatenate([a_high, a_high, a_low], axis=1),
        jnp.concatenate([b_high, b_low, b_high], axis=0),
    )


def dot3_tn(a, b):
    a_high, a_low = split3(a)
    b_high, b_low = split3(b)
    return dot_tn(
        jnp.concatenate([a_high, a_high, a_low], axis=0),
        jnp.concatenate([b_high, b_low, b_high], axis=0),
    )


def final_kernel(
    near_ref,
    far_ref,
    left_ref,
    near_matrix_ref,
    far_matrix_ref,
    warm_ref,
    q_hbm,
    update_hbm,
    error_hbm,
    q_ref,
    update_ref,
    error_ref,
    sems,
    *,
    groups,
):
    width = near_ref.shape[1]
    side = lax.axis_index("dp") % 2
    near = pl.ds(pl.multiple_of(side * width, width), width)
    far = pl.ds(pl.multiple_of((1 - side) * width, width), width)
    gram = dot_nt(near_ref[...], warm_ref[:, near], HIGHEST) + dot_nt(
        far_ref[...], warm_ref[:, far], HIGHEST
    )
    inverse = inverse_factor(gram)
    ortho = dot3_nn(inverse, left_ref[...])
    copies = []
    for half, (columns, right_ref, matrix_ref) in enumerate(
        ((near, near_ref, near_matrix_ref), (far, far_ref, far_matrix_ref))
    ):
        new_q = dot3_nn(inverse, right_ref[...]) / groups
        update = dot3_tn(ortho, new_q)
        q_ref[half] = new_q
        update_ref[half] = update
        error_ref[half] = matrix_ref[...] - update
        for part, (source, target) in enumerate(
            ((q_ref, q_hbm), (update_ref, update_hbm), (error_ref, error_hbm))
        ):
            copies.append(
                pltpu.make_async_copy(source.at[half], target.at[:, columns], sems.at[half, part])
            )
            copies[-1].start()
    for copy in copies:
        copy.wait()


def stage_order(bits, swapped):
    order = list(range(bits))
    if swapped and bits > 1:
        order[0], order[1] = 1, 0
    return order


def exchange(x, axes, size, mask):
    return lax.ppermute(x, axes, [(i, i ^ mask) for i in range(size)])


def body(
    node_state,
    edge_state,
    senders,
    receivers,
    send_index,
    cotangent,
    w_edge,
    w_node,
    error_memory,
    warm_q,
):
    node_block = node_state[0]
    edge_block = edge_state[0]
    nodes, features = node_block.shape
    edges = edge_block.shape[0]
    partitions = lax.axis_size("graph")
    replicas = lax.axis_size("dp")
    rank = warm_q.shape[1]
    warm = warm_q.T
    tile = edges // 2
    params = functools.partial(pltpu.CompilerParams, vmem_limit_bytes=24 * MIB)

    vmem = pl.BlockSpec(memory_space=pltpu.VMEM)
    hbm = pl.BlockSpec(memory_space=pltpu.HBM)
    outgoing = pl.pallas_call(
        pick_kernel,
        in_specs=[hbm] * 2,
        out_specs=vmem,
        out_shape=jax.ShapeDtypeStruct((send_index.shape[2], features), BF16),
        scratch_shapes=[
            pltpu.VMEM((1, send_index.shape[2]), jnp.int32),
            pltpu.VMEM(node_block.shape, BF16),
            pltpu.SemaphoreType.DMA((2,)),
        ],
        compiler_params=pltpu.CompilerParams(vmem_limit_bytes=60 * MIB),
    )(send_index[0], node_block)
    incoming = lax.all_to_all(
        outgoing.reshape(partitions, -1, features), "graph", split_axis=0, concat_axis=0, tiled=True
    ).reshape(-1, features)

    steps = edges // tile
    pre_type = F32
    edge_pre = pl.pallas_call(
        functools.partial(edge_kernel, tile=tile),
        in_specs=[hbm] * 5,
        out_specs=hbm,
        out_shape=jax.ShapeDtypeStruct((edges, features), pre_type),
        scratch_shapes=[
            pltpu.VMEM(senders.shape, jnp.int32),
            pltpu.VMEM(receivers.shape, jnp.int32),
            pltpu.VMEM((edges, features), BF16),
            pltpu.VMEM((nodes, features), BF16),
            pltpu.VMEM(w_edge.shape, BF16),
            pltpu.VMEM((features + 2 * nodes, features), BF16),
            pltpu.VMEM((edges, features), pre_type),
            pltpu.SemaphoreType.DMA((6,)),
            pltpu.SemaphoreType.DMA((steps,)),
            pltpu.SemaphoreType.DMA((steps,)),
        ],
        compiler_params=pltpu.CompilerParams(vmem_limit_bytes=60 * MIB),
    )(senders, receivers, edge_block, node_block, w_edge)
    rows = w_node.shape[0] // partitions
    width = features // 2
    piece = (partitions // 2, rows, width)
    new_block, near_send, near_keep, far_send, far_keep = pl.pallas_call(
        functools.partial(node_kernel, tile=tile),
        in_specs=[vmem] * 6 + [hbm] * 3,
        out_specs=[vmem] * 5,
        out_shape=[
            jax.ShapeDtypeStruct(node_block.shape, BF16),
            jax.ShapeDtypeStruct(piece, BF16),
            jax.ShapeDtypeStruct(piece, F32),
            jax.ShapeDtypeStruct(piece, BF16),
            jax.ShapeDtypeStruct(piece, F32),
        ],
        scratch_shapes=[
            pltpu.VMEM((edges, features), pre_type),
            pltpu.VMEM((edges, features), BF16),
            pltpu.VMEM((features, features), BF16),
            pltpu.VMEM(incoming.shape, BF16),
            pltpu.VMEM((nodes, features), F32),
            pltpu.VMEM((nodes, features), BF16),
            pltpu.VMEM((nodes, features), BF16),
            pltpu.VMEM(w_node.shape, F32),
            pltpu.SemaphoreType.DMA((1,)),
            pltpu.SemaphoreType.DMA((steps,)),
            pltpu.SemaphoreType.DMA((steps,)),
        ],
        compiler_params=pltpu.CompilerParams(vmem_limit_bytes=50 * MIB),
    )(
        senders,
        receivers,
        incoming,
        node_block,
        cotangent[0],
        w_node,
        edge_pre,
        edge_block,
        w_edge,
    )

    bits = partitions.bit_length() - 1
    near_order, far_order = stage_order(bits, False), stage_order(bits, True)

    def swap(x, bit):
        return exchange(x, "graph", partitions, 1 << bit)

    def halve(keep, got):
        total = keep + got.astype(F32)
        count = total.shape[-3] // 2
        return total[..., :count, :, :], total[..., count:, :, :].astype(BF16)

    near_got = swap(near_send, near_order[0])
    far_got = swap(far_send, far_order[0])
    near_keep, near_send = halve(near_keep, near_got)
    far_keep, far_send = halve(far_keep, far_got)
    near_got = swap(near_send, near_order[1])
    far_got = swap(far_send, far_order[1])
    keep = jnp.stack([near_keep, far_keep])
    got = jnp.stack([near_got, far_got])
    for bit in near_order[2:]:
        keep, send = halve(keep, got)
        got = swap(send, bit)

    near_matrix, far_matrix = pl.pallas_call(
        matrix_kernel,
        out_shape=[jax.ShapeDtypeStruct((rows, width), F32)] * 2,
        compiler_params=params(),
    )(keep, got, error_memory[0])
    mean = near_matrix + exchange(far_matrix, "dp", replicas, 1)
    mask = 2
    while 2 * mask < replicas:
        mean = mean + exchange(mean, "dp", replicas, mask)
        mask *= 2
    mean = mean.astype(BF16)
    got = exchange(mean, "dp", replicas, mask)
    total, left = pl.pallas_call(
        left_kernel,
        out_shape=[
            jax.ShapeDtypeStruct((rows, width), F32),
            jax.ShapeDtypeStruct((rank, rows), F32),
        ],
        compiler_params=params(),
    )(mean, got, warm)
    other = exchange(left, "dp", replicas, 1)
    left, right = pl.pallas_call(
        right_kernel,
        out_shape=[
            jax.ShapeDtypeStruct((rank, rows), F32),
            jax.ShapeDtypeStruct((rank, width), F32),
        ],
        compiler_params=params(),
    )(left, other, total)
    along, across = swap(right, 0), swap(right, 1)
    corner = exchange(right, "graph", partitions, 3)
    right = (right + along) + (across + corner)
    for bit in range(2, bits):
        right = right + swap(right, bit)
    far_right = exchange(right, "dp", replicas, 1)

    new_q, update, new_error = pl.pallas_call(
        functools.partial(final_kernel, groups=replicas),
        in_specs=[vmem] * 6,
        out_specs=[hbm] * 3,
        out_shape=[
            jax.ShapeDtypeStruct((rank, features), F32),
            jax.ShapeDtypeStruct((rows, features), F32),
            jax.ShapeDtypeStruct((rows, features), F32),
        ],
        scratch_shapes=[
            pltpu.VMEM((2, rank, width), F32),
            pltpu.VMEM((2, rows, width), F32),
            pltpu.VMEM((2, rows, width), F32),
            pltpu.SemaphoreType.DMA((2, 3)),
        ],
        compiler_params=params(),
    )(right, far_right, left, near_matrix, far_matrix, warm)
    return (new_block[None], update, new_error[None], new_q.T)


def solution(mesh):
    return jax.shard_map(
        body,
        mesh=mesh,
        in_specs=(
            P("dp", "graph", None),
            P("dp", "graph", None),
            P("dp", "graph"),
            P("dp", "graph"),
            P("dp", "graph", None),
            P("dp", "graph", None),
            P(),
            P(),
            P("dp", "graph", None),
            P(),
        ),
        out_specs=(P("dp", "graph", None), P("graph", None), P("dp", "graph", None), P()),
        check_vma=False,
    )
```
